32 devices in a mesh: sub: 8 (over z, y), iter: 4 (over x, core).
Axes of the slice: x: 2, y: 2, z: 4, core: 2. Of those that a mesh axis runs over, the one named last changes fastest.
Arguments:
- fields: float32 [4, 16, 128, 128], P('iter', 'sub'), may hold values from -6 to 6
- labels: int32 [16, 128, 128], P('sub'), may hold values from 0 to 3
- traces: float32 [4, 8, 4, 128, 128], P('iter', 'sub'), may hold values from -6 to 6
- new_guess: float32 [2, 8, 4, 128, 128], P(None, 'sub'), may hold values from -6 to 6
- cond_table: float32 [4], replicated, may hold values from 0.2 to 5
- cap_table: float32 [4], replicated, may hold values from 0.5 to 4
Outputs:
- end_fields: float32 [4, 16, 128, 128], P('iter', 'sub')
- corrected: float32 [4, 8, 4, 128, 128], P('iter', 'sub')
The draws below stay inside these ranges and needn't reach their ends.
All inputs are finite; a program needn't handle non-finite values.
Results may differ from the reference program's by a relative error of at most 0.00002.
Values sent between devices are 32-bit elements; how exact they have to be, the bound alone decides.
No kernel may reach another device: no remote copies, remote signals or barrier semaphores. Data moves between devices by JAX's collectives and lax.ppermute only.
A program may use at most 64 MiB of HBM per device.

```python
import math
import jax
import jax.numpy as jnp

CX = 2
NY = 128
NZ = 128
STEPS = 4
SWEEPS = 3
TICKS = 3
CLASSES = 4
GROUPS = 4
NX = 16
N_SUB = 8


def set_ends(entries, rng, low, largest):
    longest = entries.shape.index(max(entries.shape))
    spots = []
    for shift in (0, 1):
        where = [jax.random.randint(jax.random.fold_in(rng, axis), (), 0, length) for axis, length in enumerate(entries.shape)]
        where[longest] = (where[longest] + shift) % entries.shape[longest]
        spots.append(tuple(where))
    return entries.at[spots[0]].set(low).at[spots[1]].set(largest)


def block_scale(own_key, extent, split, smallest, top_value):
    def one(position, parts):
        draws = jax.random.uniform(jax.random.fold_in(jax.random.fold_in(own_key, 6), position), (parts,), jnp.float32, smallest / len(split), top_value / len(split))
        return jnp.repeat(jnp.exp(draws), extent[position] // parts).reshape((-1,) + (1,) * (len(extent) - position - 1))

    factor_of = one(*split[0])
    for cut in split[1:]:
        factor_of = factor_of * one(*cut)
    return factor_of


def scatter_about(rng, shape, width, limit, pieces=(), kind=jnp.bfloat16):
    values = width * jax.random.normal(rng, shape, jnp.float32)
    if pieces:
        values = values * block_scale(rng, shape, pieces, -0.22, 0.18)
    return jnp.clip(values, -limit, limit).astype(kind)


def setup_inputs(seed: int = 0) -> dict:
    seeds = jax.random.split(jax.random.key(seed), 7)
    fields = scatter_about(seeds[0], (GROUPS, NX, NY, NZ), 1.0, 6.0, ((0, 4), (1, 8)), jnp.float32)
    labels = set_ends(jax.random.randint(seeds[1], (NX, NY, NZ), 0, CLASSES), jax.random.fold_in(seeds[1], 1), 0, CLASSES - 1).astype(jnp.int32)
    traces = scatter_about(seeds[2], (GROUPS, N_SUB, STEPS, NY, NZ), 1.0, 6.0, ((0, 4), (1, 8)), jnp.float32)
    new_guess = scatter_about(seeds[3], (TICKS - 1, N_SUB, STEPS, NY, NZ), 1.0, 6.0, ((1, 8),), jnp.float32)
    cond_table = jnp.clip(jnp.exp(jax.random.uniform(seeds[4], (CLASSES,), jnp.float32, math.log(0.2), math.log(5.0))), 0.2, 5.0)
    cap_table = jnp.clip(jnp.exp(jax.random.uniform(seeds[5], (CLASSES,), jnp.float32, math.log(0.5), math.log(4.0))), 0.5, 4.0)
    return {"fields": fields, "labels": labels, "traces": traces, "new_guess": new_guess, "cond_table": cond_table, "cap_table": cap_table}


def harmonic(first, second):
    return 2.0 * first * second / (first + second)


def setup(labels, cond_table, cap_table, left_mask, right_mask):
    conduct = jnp.zeros(labels.shape, jnp.float32)
    capacity = jnp.zeros(labels.shape, jnp.float32)
    for cls in range(cond_table.shape[0]):
        hit = labels == cls
        conduct = jnp.where(hit, cond_table[cls], conduct)
        capacity = jnp.where(hit, cap_table[cls], capacity)
    face_x = harmonic(conduct[:, 1:], conduct[:, :-1])
    face_y = harmonic(conduct[:, :, 1:], conduct[:, :, :-1])
    face_z = harmonic(conduct[:, :, :, 1:], conduct[:, :, :, :-1])
    end_first = 2.0 * conduct[:, 0]
    end_last = 2.0 * conduct[:, -1]
    sum_x = jnp.pad(face_x, ((0, 0), (1, 0), (0, 0), (0, 0))) + jnp.pad(face_x, ((0, 0), (0, 1), (0, 0), (0, 0)))
    sum_x = sum_x.at[:, 0].add(end_first).at[:, -1].add(end_last)
    sum_y = jnp.pad(face_y, ((0, 0), (0, 0), (1, 0), (0, 0))) + jnp.pad(face_y, ((0, 0), (0, 0), (0, 1), (0, 0)))
    sum_y = sum_y.at[:, :, 0].add(2.0 * conduct[:, :, 0]).at[:, :, -1].add(2.0 * conduct[:, :, -1])
    sum_z = jnp.pad(face_z, ((0, 0), (0, 0), (0, 0), (1, 0))) + jnp.pad(face_z, ((0, 0), (0, 0), (0, 0), (0, 1)))
    sum_z = sum_z.at[:, :, :, 0].add(2.0 * conduct[:, :, :, 0]).at[:, :, :, -1].add(2.0 * conduct[:, :, :, -1])
    diag_d = capacity + sum_x + sum_y + sum_z
    diag_n = diag_d.at[:, 0].add(-left_mask[:, None, None] * end_first)
    diag_n = diag_n.at[:, -1].add(-right_mask[:, None, None] * end_last)
    return capacity, face_x, face_y, face_z, end_first, end_last, diag_d, diag_n


def relax(value, rhs, diag, face_x, face_y, face_z):
    for sweep in range(SWEEPS):
        near = jnp.pad(face_x * value[:, :-1], ((0, 0), (1, 0), (0, 0), (0, 0)))
        near = near + jnp.pad(face_x * value[:, 1:], ((0, 0), (0, 1), (0, 0), (0, 0)))
        near = near + jnp.pad(face_y * value[:, :, :-1], ((0, 0), (0, 0), (1, 0), (0, 0)))
        near = near + jnp.pad(face_y * value[:, :, 1:], ((0, 0), (0, 0), (0, 1), (0, 0)))
        near = near + jnp.pad(face_z * value[:, :, :, :-1], ((0, 0), (0, 0), (0, 0), (1, 0)))
        near = near + jnp.pad(face_z * value[:, :, :, 1:], ((0, 0), (0, 0), (0, 0), (0, 1)))
        value = (rhs + near) / diag
    return value


def dirichlet(state, left_trace, right_trace, coeffs):
    capacity, face_x, face_y, face_z, end_first, end_last, diag_d, diag_n = coeffs
    firsts = []
    lasts = []
    for step in range(left_trace.shape[1]):
        rhs = capacity * state
        rhs = rhs.at[:, 0].add(end_first * left_trace[:, step])
        rhs = rhs.at[:, -1].add(end_last * right_trace[:, step])
        state = relax(state, rhs, diag_d, face_x, face_y, face_z)
        firsts.append(state[:, 0])
        lasts.append(state[:, -1])
    return state, jnp.stack(firsts, axis=1), jnp.stack(lasts, axis=1)


def neumann(left_jump, right_jump, coeffs):
    capacity, face_x, face_y, face_z, end_first, end_last, diag_d, diag_n = coeffs
    psi = jnp.zeros(diag_n.shape, jnp.float32)
    firsts = []
    lasts = []
    for step in range(left_jump.shape[1]):
        rhs = capacity * psi
        rhs = rhs.at[:, 0].add(left_jump[:, step])
        rhs = rhs.at[:, -1].add(right_jump[:, step])
        psi = relax(psi, rhs, diag_n, face_x, face_y, face_z)
        firsts.append(psi[:, 0])
        lasts.append(psi[:, -1])
    return jnp.stack(firsts, axis=1), jnp.stack(lasts, axis=1)


def shift_right(planes):
    return jnp.concatenate([jnp.zeros_like(planes[:1]), planes[:-1]], axis=0)


def shift_left(planes):
    return jnp.concatenate([planes[1:], jnp.zeros_like(planes[:1])], axis=0)


def reference(fields, labels, traces, new_guess, cond_table, cap_table):
    slabs = N_SUB
    slab_pos = jnp.arange(slabs)
    left_mask = (slab_pos > 0).astype(jnp.float32)
    right_mask = (slab_pos < slabs - 1).astype(jnp.float32)
    right_wide = right_mask[:, None, None, None]
    coeffs = setup(labels.reshape(slabs, CX, NY, NZ), cond_table, cap_table, left_mask, right_mask)
    end_first, end_last = coeffs[4], coeffs[5]
    states = [fields[group].reshape(slabs, CX, NY, NZ) for group in range(GROUPS)]
    rights = [traces[group] * right_wide for group in range(GROUPS)]
    results = []
    for tick in range(TICKS):
        results = []
        for group in range(GROUPS):
            right_trace = rights[group]
            left_trace = shift_right(right_trace)
            state, firsts, lasts = dirichlet(states[group], left_trace, right_trace, coeffs)
            states[group] = state
            q_first = end_first[:, None] * (firsts - left_trace)
            q_last = end_last[:, None] * (lasts - right_trace)
            right_jump = (q_last + shift_left(q_first)) * right_wide
            left_jump = shift_right(right_jump)
            psi_first, psi_last = neumann(left_jump, right_jump, coeffs)
            results.append((right_trace + 0.25 * (psi_last + shift_left(psi_first))) * right_wide)
        if tick + 1 < TICKS:
            rights = [new_guess[tick] * right_wide] + results[:-1]
    end_fields = jnp.stack([state.reshape(NX, NY, NZ) for state in states])
    return end_fields, jnp.stack(results)
```

```python
import functools

import jax
import jax.numpy as jnp
from jax import lax
from jax.experimental import pallas as pl
from jax.experimental.pallas import tpu as pltpu
from jax.sharding import PartitionSpec as P

SWEEPS = 3
AXES = ("sub", "iter")
F32 = jnp.float32
PAD = 8
SPLIT = 1
LIMIT = 8 << 20


def vmem(shape, dtype=F32):
    return pltpu.VMEM(shape, dtype)


def near(value):
    return pltpu.with_memory_space_constraint(value, pltpu.VMEM)


def harmonic(first, second):
    return 2.0 * first * second / (first + second)


class Layout:
    def __init__(self, slabs, groups):
        assert slabs % 2 == 0 and groups % 2 == 0
        self.slabs, self.groups = slabs, groups
        every = [(s, p) for s in range(slabs) for p in range(groups)]
        at = self.at
        self.core = [(at(s, p), at(s ^ 1, p)) for s, p in every]
        self.chip = []
        for s, p in every:
            t = s + 1 if s % 2 else s - 1
            self.chip.append((at(s, p), at(t, p) if 0 <= t < slabs else at(s, (p + 2) % groups)))
        self.field = [(at(s, p), at(s, (p - 1) % groups)) for s, p in every]
        self.enter = []
        self.guess = []
        for s, g in every:
            here = s * groups + g
            if s % 2 != g % 2:
                there = (s ^ 1) * groups + (g ^ 1)
            else:
                there = s * groups + (g + 2) % groups
            self.enter.append((here, there))
            self.guess.append((here, (s ^ 1) * groups + g))

    def at(self, s, p):
        return (2 * (s // 2) + p % 2) * self.groups + 2 * (p // 2) + s % 2

    def home(self, ticks):
        every = [(s, p) for s in range(self.slabs) for p in range(self.groups)]
        return [(self.at(s, p), s * self.groups + (p + ticks - 1) % self.groups) for s, p in every]


def place():
    sub, it = lax.axis_index("sub"), lax.axis_index("iter")
    parity = lax.rem(it, 2)
    slab = 2 * (sub // 2) + parity
    position = 2 * (it // 2) + lax.rem(sub, 2)
    return parity, slab, position


def has_far():
    parity, slab, _ = place()
    last = lax.axis_size("sub") - 1
    return jnp.logical_not(jnp.where(parity == 0, slab == 0, slab == last))


def stays():
    return lax.rem(lax.axis_index("sub"), 2) == lax.rem(lax.axis_index("iter"), 2)


def flipped(plane, planes, parity):
    return plane + parity * (planes - 1 - 2 * plane)


def row_cap(p):
    return 5 * p


def row_face(planes, f):
    return 5 * planes + 2 * f


def row_end(planes, role_a):
    return 5 * planes + 2 * (planes - 1) + role_a


def rows(planes):
    return 5 * planes + 2 * (planes - 1) + 2


def setup_kernel(cond_ref, cap_ref, mine_ref, other_ref, dir_ref, neu_ref, end_ref):
    planes, ny, nz = mine_ref.shape
    parity, _, _ = place()
    keep = stays()
    far = has_far()
    row = lax.broadcasted_iota(jnp.int32, (ny, nz), 0)
    col = lax.broadcasted_iota(jnp.int32, (ny, nz), 1)
    ks, cs = [], []
    for p in range(planes):
        at = flipped(p, planes, parity)
        label = jnp.where(keep, mine_ref[at], other_ref[at])
        k = jnp.zeros((ny, nz), F32)
        c = jnp.zeros((ny, nz), F32)
        for cls in range(cond_ref.shape[0]):
            hit = label == cls
            k = jnp.where(hit, cond_ref[cls], k)
            c = jnp.where(hit, cap_ref[cls], c)
        ks.append(k)
        cs.append(c)
    faces = [harmonic(ks[f], ks[f + 1]) for f in range(planes - 1)]
    end_ref[0] = 2.0 * ks[0]
    end_ref[1] = 2.0 * ks[-1]
    for p in range(planes):
        k = ks[p]
        down = harmonic(k, pltpu.roll(k, ny - 1, 0))
        up = pltpu.roll(down, 1, 0)
        right = harmonic(k, pltpu.roll(k, nz - 1, 1))
        left = pltpu.roll(right, 1, 1)
        edge = 2.0 * k
        total = cs[p]
        total = total + ((faces[p - 1] if p else edge) + (faces[p] if p < planes - 1 else edge))
        total = total + (jnp.where(row == 0, edge, up) + jnp.where(row == ny - 1, edge, down))
        total = total + (jnp.where(col == 0, edge, left) + jnp.where(col == nz - 1, edge, right))
        up = jnp.where(row == 0, 0.0, up)
        down = jnp.where(row == ny - 1, 0.0, down)
        left = jnp.where(col == 0, 0.0, left)
        right = jnp.where(col == nz - 1, 0.0, right)
        free = total
        if p == 0:
            free = free - jnp.where(far, edge, 0.0)
        if p == planes - 1:
            free = free - edge
        for out, diag in ((dir_ref, total), (neu_ref, free)):
            inverse = 1.0 / diag
            for n, value in enumerate((cs[p], up, down, left, right)):
                out[row_cap(p) + n] = value * inverse
            if p < planes - 1:
                out[row_face(planes, p)] = faces[p] * inverse
            if p:
                out[row_face(planes, p - 1) + 1] = faces[p - 1] * inverse
            weight = edge * inverse if out is dir_ref else inverse
            if p == 0:
                out[row_end(planes, 0)] = weight
            if p == planes - 1:
                out[row_end(planes, 1)] = weight


def clear_pads(refs):
    for ref in refs:
        planes, tall, nz = ref.shape
        for p in range(planes):
            ref[p, 0:PAD, :] = jnp.zeros((PAD, nz), F32)
            ref[p, tall - PAD : tall, :] = jnp.zeros((PAD, nz), F32)


def sweep(coef, source, target, rhs):
    planes, tall, nz = source.shape
    for r in range(0, tall - 2 * PAD, 8):
        here = slice(r, r + 8)
        xs = [source[p, PAD + r : PAD + r + 8, :] for p in range(planes)]
        for p in range(planes):
            x = xs[p]
            base = row_cap(p)
            value = rhs(p, here, x)
            if p < planes - 1:
                value = value + coef[row_face(planes, p), here, :] * xs[p + 1]
            if p:
                value = value + coef[row_face(planes, p - 1) + 1, here, :] * xs[p - 1]
            side = coef[base + 1, here, :] * source[p, PAD + r - 1 : PAD + r + 7, :]
            side = side + coef[base + 2, here, :] * source[p, PAD + r + 1 : PAD + r + 9, :]
            value = value + side
            side = coef[base + 3, here, :] * pltpu.roll(x, 1, 1)
            side = side + coef[base + 4, here, :] * pltpu.roll(x, nz - 1, 1)
            target(p, here, value + side)


def padded(here):
    return slice(here.start + PAD, here.stop + PAD)


def solve(coef, buffers, hold, first_rhs, final, known_zero=False):
    planes, tall, nz = buffers[0].shape

    for n in range(SWEEPS):
        source, target = buffers

        def rhs(p, here, x):
            if n:
                return hold[p, here, :]
            value = first_rhs(p, here, x)
            hold[p, here, :] = value
            return value

        def put(p, here, value):
            target[p, padded(here), :] = value
            if n == SWEEPS - 1:
                final(p, here, value)

        if n == 0 and known_zero:
            for r in range(0, tall - 2 * PAD, 8):
                for p in range(planes):
                    here = slice(r, r + 8)
                    put(p, here, rhs(p, here, None))
        else:
            sweep(coef, source, put, rhs)
        buffers = buffers[::-1]
    return buffers


def dirichlet_kernel(lo, start, enter, fresh, out_native, *refs):
    refs = list(refs)
    take = lambda n: [refs.pop(0) for _ in range(n)]
    coef, end = take(2)
    parity, _, position = place()
    far = has_far()
    if enter:
        keep = stays()
        mine, other = take(2)
    else:
        (field,) = take(1)
    if start:
        held, from_core, from_chip = take(3)
    else:
        old_a, old_b, psi_a, psi_b, got_a, got_b, ng, gy = take(8)
    out_field, out_qa, out_qb, out_ha, out_hb, va, vb, hold = take(8)
    planes = va.shape[0]
    steps = out_qa.shape[0]
    ny = out_qa.shape[1]
    clear_pads((va, vb))
    for p in range(planes):
        if enter:
            at = flipped(p, planes, parity)
            value = jnp.where(keep, mine[0, at], other[0, at])
        else:
            value = field[p]
        va[p, PAD : PAD + ny, :] = value
    for n in range(steps):
        if start:
            h_a = jnp.where(parity == 0, held[n], from_core[n])
            h_b = jnp.where(parity == 0, from_chip[n], held[n])
        else:
            h_a = old_a[n] + 0.25 * (psi_a[n] + got_a[n])
            h_b = old_b[n] + 0.25 * (psi_b[n] + got_b[n])
            groups = lax.axis_size("iter")
            begins = (groups - fresh) % groups
            new = position == begins
            local, crossed = ng[fresh - 1, 0, lo + n], gy[lo + n]
            near_a, near_b = (crossed, local) if begins % 2 else (local, crossed)
            h_a = jnp.where(new, near_a, h_a)
            h_b = jnp.where(new, jnp.where(parity == 1, near_b, got_b[n]), h_b)
        out_ha[n] = h_a
        out_hb[n] = jnp.where(far, h_b, 0.0)
    buffers = [va, vb]
    for n in range(steps):

        def first_rhs(p, here, x):
            value = coef[row_cap(p), here, :] * x
            if p == 0:
                value = value + coef[row_end(planes, 0), here, :] * out_hb[n, here, :]
            if p == planes - 1:
                value = value + coef[row_end(planes, 1), here, :] * out_ha[n, here, :]
            return value

        def final(p, here, value):
            if p == 0:
                out_qb[n, here, :] = end[0, here, :] * (value - out_hb[n, here, :])
            if p == planes - 1:
                out_qa[n, here, :] = end[1, here, :] * (value - out_ha[n, here, :])

        buffers = solve(coef, buffers, hold, first_rhs, final)
    for p in range(planes):
        value = buffers[0][p, PAD : PAD + ny, :]
        if out_native:
            out_field[flipped(p, planes, parity)] = value
        else:
            out_field[p] = value


def neumann_kernel(lo, first, fresh, *refs):
    refs = list(refs)
    take = lambda n: [refs.pop(0) for _ in range(n)]
    (coef,) = take(1)
    parity, _, position = place()
    far = has_far()
    q_a, q_b, got_a, got_b = take(4)
    if not first:
        (state,) = take(1)
    if fresh:
        ng, gy = take(2)
    out_state, out_a, out_b, va, vb, hold = take(6)
    planes = va.shape[0]
    steps, ny, nz = out_a.shape
    clear_pads((va, vb))
    if not first:
        for p in range(planes):
            va[p, PAD : PAD + ny, :] = state[p]
    buffers = [va, vb]
    for n in range(steps):
        zero = first and n == 0

        def first_rhs(p, here, x):
            value = jnp.zeros((8, nz), F32) if zero else coef[row_cap(p), here, :] * x
            if p == 0:
                jump = jnp.where(far, q_b[n, here, :] + got_b[n, here, :], 0.0)
                value = value + coef[row_end(planes, 0), here, :] * jump
            if p == planes - 1:
                jump = q_a[n, here, :] + got_a[n, here, :]
                value = value + coef[row_end(planes, 1), here, :] * jump
            return value

        def final(p, here, value):
            if p == 0:
                out_b[n, here, :] = value
            if p == planes - 1:
                out_a[n, here, :] = value

        buffers = solve(coef, buffers, hold, first_rhs, final, known_zero=zero)
    for p in range(planes):
        out_state[p] = buffers[0][p, PAD : PAD + ny, :]
    if fresh:
        groups = lax.axis_size("iter")
        begins = (groups - fresh) % groups

        @pl.when(position == begins)
        def _():
            for n in range(steps):
                out_b[n] = ng[fresh - 1, 0, lo + n] if begins % 2 else gy[lo + n]


def correct_kernel(h_a, h_b, psi_a, psi_b, got_a, got_b, out):
    parity, _, _ = place()
    far = has_far()

    @pl.when(parity == 0)
    def _():
        out[...] = h_a[...] + 0.25 * (psi_a[...] + got_a[...])

    @pl.when(parity == 1)
    def _():
        out[...] = jnp.where(far, h_b[...] + 0.25 * (psi_b[...] + got_b[...]), 0.0)


def hold_kernel(mine, other, out):
    keep = stays()
    out[...] = jnp.where(keep, mine[0, 0], other[0, 0])


def run(kernel, outs, args, scratch=(), name=None, smem=0):
    specs = [pl.BlockSpec(memory_space=pltpu.SMEM)] * smem
    specs += [pl.BlockSpec(memory_space=pltpu.VMEM)] * (len(args) - smem)
    many = isinstance(outs, tuple)
    return pl.pallas_call(
        kernel,
        out_shape=outs,
        in_specs=specs,
        out_specs=tuple([pl.BlockSpec(memory_space=pltpu.VMEM)] * len(outs)) if many else specs[-1],
        scratch_shapes=list(scratch),
        compiler_params=pltpu.CompilerParams(vmem_limit_bytes=LIMIT),
        name=name,
    )(*args[:smem], *[near(a) for a in args[smem:]])


def local(layout, fields, labels, traces, new_guess, cond_table, cap_table):
    move = lambda value, pairs: lax.ppermute(value, AXES, pairs)
    planes, ny, nz = labels.shape
    steps = traces.shape[2]
    ticks = new_guess.shape[0] + 1
    groups = layout.groups
    odd = lax.rem(lax.axis_index("sub"), 2)
    size = max(1, steps // SPLIT)
    chunks = [(lo, min(lo + size, steps)) for lo in range(0, steps, size)]
    scratch = [vmem((planes, ny + 2 * PAD, nz))] * 2 + [vmem((planes, ny, nz))]

    got_traces = move(traces, layout.enter)
    got_labels = move(labels, layout.enter)
    got_fields = move(fields, layout.enter)
    held = run(hold_kernel, vmem((steps, ny, nz)), [traces, got_traces], name="held")
    from_core = move(held, layout.core)
    from_chip = move(held, layout.chip)
    count = rows(planes)
    dir_coef, neu_coef, end = run(
        setup_kernel,
        (vmem((count, ny, nz)), vmem((count, ny, nz)), vmem((2, ny, nz))),
        [cond_table, cap_table, labels, got_labels],
        name="setup",
        smem=2,
    )

    starts = {t: (groups - t) % groups for t in range(1, ticks)}
    odds = [t for t in starts if starts[t] % 2]
    evens = [t for t in starts if starts[t] % 2 == 0]
    crossed = {}
    for n in range(max(len(odds), len(evens))):
        ours = odds[n] if n < len(odds) else evens[n]
        theirs = evens[n] if n < len(evens) else odds[n]
        message = jnp.where(odd == 0, new_guess[ours - 1, 0], new_guess[theirs - 1, 0])
        arrived = move(message, layout.guess)
        crossed[ours] = crossed[theirs] = arrived

    field = None
    state = None
    waves = None
    for tick in range(ticks):
        last = tick == ticks - 1
        sent = []
        for lo, hi in chunks:
            m = hi - lo
            args = [dir_coef, end]
            enter = tick == 0 and lo == 0
            args += [fields, got_fields] if enter else [field]
            if tick == 0:
                args += [a[lo:hi] for a in (held, from_core, from_chip)] if len(chunks) > 1 else [held, from_core, from_chip]
            else:
                args += [*waves[lo], new_guess, crossed[tick]]
            plane = vmem((m, ny, nz))
            field, q_a, q_b, h_a, h_b = run(
                functools.partial(dirichlet_kernel, lo, tick == 0, enter, tick, last and hi == steps),
                (vmem((planes, ny, nz)), plane, plane, plane, plane),
                args,
                scratch,
                name=f"dirichlet_{tick}_{lo}",
            )
            sent.append((q_a, q_b, move(q_a, layout.core), move(q_b, layout.chip), h_a, h_b))
        field = move(field[None] if last else field, layout.home(ticks) if last else layout.field)
        fresh = 0 if last else tick + 1
        waves = {}
        state = None
        ends = []
        for (lo, hi), (q_a, q_b, got_a, got_b, h_a, h_b) in zip(chunks, sent):
            m = hi - lo
            args = [neu_coef, q_a, q_b, got_a, got_b]
            if lo:
                args.append(state)
            if fresh:
                args += [new_guess, crossed[fresh]]
            plane = vmem((m, ny, nz))
            state, psi_a, psi_b = run(
                functools.partial(neumann_kernel, lo, lo == 0, fresh),
                (vmem((planes, ny, nz)), plane, plane),
                args,
                scratch,
                name=f"neumann_{tick}_{lo}",
            )
            in_a = move(psi_a, layout.core)
            in_b = move(psi_b, layout.chip)
            waves[lo] = (h_a, h_b, psi_a, psi_b, in_a, in_b)
            if last:
                done = run(correct_kernel, plane, list(waves[lo]), name=f"correct_{lo}")
                ends.append(move(done, layout.home(ticks)))
    corrected = ends[0] if len(ends) == 1 else jnp.concatenate(ends, axis=0)
    return field, corrected[None, None]


def solution(mesh):
    layout = Layout(mesh.shape["sub"], mesh.shape["iter"])
    return jax.shard_map(
        functools.partial(local, layout),
        mesh=mesh,
        in_specs=(
            P("iter", "sub", None, None),
            P("sub", None, None),
            P("iter", "sub", None, None, None),
            P(None, "sub", None, None, None),
            P(),
            P(),
        ),
        out_specs=(P("iter", "sub", None, None), P("iter", "sub", None, None, None)),
        check_vma=False,
    )
```

```python
import functools

import jax
import jax.numpy as jnp
from jax import lax
from jax.experimental import pallas as pl
from jax.experimental.pallas import tpu as pltpu
from jax.sharding import PartitionSpec as P


SWEEPS = 3
AXES = ("sub", "iter")
F32 = jnp.float32
PAD = 8
SPLIT = 2
LIMIT = 8 << 20


def vmem(shape, dtype=F32):
    return pltpu.VMEM(shape, dtype)


def near(value):
    return pltpu.with_memory_space_constraint(value, pltpu.VMEM)


def harmonic(first, second):
    return 2.0 * first * second / (first + second)


class Layout:
    def __init__(self, slabs, groups):
        assert slabs % 2 == 0 and groups % 2 == 0
        self.slabs, self.groups = slabs, groups
        every = [(s, p) for s in range(slabs) for p in range(groups)]
        at = self.at
        self.core = [(at(s, p), at(s ^ 1, p)) for s, p in every]
        self.chip = []
        for s, p in every:
            t = s + 1 if s % 2 else s - 1
            self.chip.append((at(s, p), at(t, p) if 0 <= t < slabs else at(s, (p + 2) % groups)))
        self.field = [(at(s, p), at(s, (p - 1) % groups)) for s, p in every]
        self.enter = [(s * groups + g, at(s, (g - 1) % groups)) for s, g in every]
        self.guess = []
        for s, g in every:
            there = s + 1 if s % 2 == 0 else (s - 1 if g % 2 else (s + 1) % slabs)
            self.guess.append((s * groups + g, there * groups + g))

    def at(self, s, p):
        return (2 * (s // 2) + p % 2) * self.groups + 2 * (p // 2) + s % 2

    def home(self, ticks):
        every = [(s, p) for s in range(self.slabs) for p in range(self.groups)]
        return [(self.at(s, p), s * self.groups + (p + ticks) % self.groups) for s, p in every]


def place():
    sub, it = lax.axis_index("sub"), lax.axis_index("iter")
    parity = lax.rem(it, 2)
    slab = 2 * (sub // 2) + parity
    position = 2 * (it // 2) + lax.rem(sub, 2)
    return parity, slab, position


def has_far():
    parity, slab, _ = place()
    last = lax.axis_size("sub") - 1
    return jnp.logical_not(jnp.where(parity == 0, slab == 0, slab == last))


def flipped(plane, planes, parity):
    return plane + parity * (planes - 1 - 2 * plane)


def row_cap(p):
    return 5 * p


def row_face(planes, f):
    return 5 * planes + 2 * f


def row_end(planes, role_a):
    return 5 * planes + 2 * (planes - 1) + role_a


def rows(planes):
    return 5 * planes + 2 * (planes - 1) + 2


def setup_kernel(cond_ref, cap_ref, label_ref, dir_ref, neu_ref, end_ref):
    planes, ny, nz = label_ref.shape
    parity, _, _ = place()
    far = has_far()
    row = lax.broadcasted_iota(jnp.int32, (ny, nz), 0)
    col = lax.broadcasted_iota(jnp.int32, (ny, nz), 1)
    ks, cs = [], []
    for p in range(planes):
        at = flipped(p, planes, parity)
        label = label_ref[at]
        k = jnp.zeros((ny, nz), F32)
        c = jnp.zeros((ny, nz), F32)
        for cls in range(cond_ref.shape[0]):
            hit = label == cls
            k = jnp.where(hit, cond_ref[cls], k)
            c = jnp.where(hit, cap_ref[cls], c)
        ks.append(k)
        cs.append(c)
    faces = [harmonic(ks[f], ks[f + 1]) for f in range(planes - 1)]
    end_ref[0] = 2.0 * ks[0]
    end_ref[1] = 2.0 * ks[-1]
    for p in range(planes):
        k = ks[p]
        down = harmonic(k, pltpu.roll(k, ny - 1, 0))
        up = pltpu.roll(down, 1, 0)
        right = harmonic(k, pltpu.roll(k, nz - 1, 1))
        left = pltpu.roll(right, 1, 1)
        edge = 2.0 * k
        total = cs[p]
        total = total + ((faces[p - 1] if p else edge) + (faces[p] if p < planes - 1 else edge))
        total = total + (jnp.where(row == 0, edge, up) + jnp.where(row == ny - 1, edge, down))
        total = total + (jnp.where(col == 0, edge, left) + jnp.where(col == nz - 1, edge, right))
        up = jnp.where(row == 0, 0.0, up)
        down = jnp.where(row == ny - 1, 0.0, down)
        left = jnp.where(col == 0, 0.0, left)
        right = jnp.where(col == nz - 1, 0.0, right)
        free = total
        if p == 0:
            free = free - jnp.where(far, edge, 0.0)
        if p == planes - 1:
            free = free - edge
        for out, diag in ((dir_ref, total), (neu_ref, free)):
            inverse = 1.0 / diag
            for n, value in enumerate((cs[p], up, down, left, right)):
                out[row_cap(p) + n] = value * inverse
            if p < planes - 1:
                out[row_face(planes, p)] = faces[p] * inverse
            if p:
                out[row_face(planes, p - 1) + 1] = faces[p - 1] * inverse
            weight = edge * inverse if out is dir_ref else inverse
            if p == 0:
                out[row_end(planes, 0)] = jnp.where(far, weight, 0.0)
            if p == planes - 1:
                out[row_end(planes, 1)] = weight


def clear_pads(refs):
    for ref in refs:
        planes, tall, nz = ref.shape
        for p in range(planes):
            ref[p, 0:PAD, :] = jnp.zeros((PAD, nz), F32)
            ref[p, tall - PAD : tall, :] = jnp.zeros((PAD, nz), F32)


def sweep(coef, source, target, rhs):
    planes, tall, nz = source.shape
    for r in range(0, tall - 2 * PAD, 8):
        here = slice(r, r + 8)
        xs = [source[p, PAD + r : PAD + r + 8, :] for p in range(planes)]
        for p in range(planes):
            x = xs[p]
            base = row_cap(p)
            value = rhs(p, here, x)
            if p < planes - 1:
                value = value + coef[row_face(planes, p), here, :] * xs[p + 1]
            if p:
                value = value + coef[row_face(planes, p - 1) + 1, here, :] * xs[p - 1]
            side = coef[base + 1, here, :] * source[p, PAD + r - 1 : PAD + r + 7, :]
            side = side + coef[base + 2, here, :] * source[p, PAD + r + 1 : PAD + r + 9, :]
            value = value + side
            side = coef[base + 3, here, :] * pltpu.roll(x, 1, 1)
            side = side + coef[base + 4, here, :] * pltpu.roll(x, nz - 1, 1)
            target(p, here, value + side)


def padded(here):
    return slice(here.start + PAD, here.stop + PAD)


def solve(coef, buffers, hold, first_rhs, final, known_zero=False):
    planes, tall, _ = buffers[0].shape

    for n in range(SWEEPS):
        source, target = buffers

        def rhs(p, here, x):
            if n:
                return hold[p, here, :]
            value = first_rhs(p, here, x)
            hold[p, here, :] = value
            return value

        def put(p, here, value):
            target[p, padded(here), :] = value
            if n == SWEEPS - 1:
                final(p, here, value)

        if n == 0 and known_zero:
            for r in range(0, tall - 2 * PAD, 8):
                for p in range(planes):
                    here = slice(r, r + 8)
                    put(p, here, rhs(p, here, None))
        else:
            sweep(coef, source, put, rhs)
        buffers = buffers[::-1]
    return buffers


def dirichlet_kernel(lo, start, enter, fresh, out_native, *refs):
    refs = list(refs)
    take = lambda n: [refs.pop(0) for _ in range(n)]
    coef, end = take(2)
    parity, _, position = place()
    far = has_far()
    (field,) = take(1)
    if start:
        held, from_core, from_chip = take(3)
    else:
        old_a, old_b, psi_a, psi_b, got_a, got_b, ng, gy = take(8)
    out_field, out_qa, out_qb, out_ha, out_hb, va, vb, hold = take(8)
    planes = va.shape[0]
    steps = out_qa.shape[0]
    ny = out_qa.shape[1]
    clear_pads((va, vb))
    for p in range(planes):
        if enter:
            value = field[0, flipped(p, planes, parity)]
        else:
            value = field[p]
        va[p, PAD : PAD + ny, :] = value
    for n in range(steps):
        if start:
            h_a = jnp.where(parity == 0, held[n], from_core[n])
            h_b = jnp.where(parity == 0, from_chip[n], held[n])
        else:
            h_a = old_a[n] + 0.25 * (psi_a[n] + got_a[n])
            h_b = old_b[n] + 0.25 * (psi_b[n] + got_b[n])
            groups = lax.axis_size("iter")
            begins = (-fresh - 1) % groups
            new = position == begins
            local, crossed = ng[fresh - 1, 0, lo + n], gy[lo + n]
            near_a, near_b = (crossed, local) if begins % 2 else (local, crossed)
            h_a = jnp.where(new, near_a, h_a)
            if begins % 2:
                near_b = jnp.where(parity == 1, near_b, got_b[n])
            h_b = jnp.where(new, near_b, h_b)
        out_ha[n] = h_a
        out_hb[n] = jnp.where(far, h_b, 0.0)
    buffers = [va, vb]
    for n in range(steps):

        def first_rhs(p, here, x):
            value = coef[row_cap(p), here, :] * x
            if p == 0:
                value = value + coef[row_end(planes, 0), here, :] * out_hb[n, here, :]
            if p == planes - 1:
                value = value + coef[row_end(planes, 1), here, :] * out_ha[n, here, :]
            return value

        def final(p, here, value):
            if p == 0:
                out_qb[n, here, :] = end[0, here, :] * (value - out_hb[n, here, :])
            if p == planes - 1:
                out_qa[n, here, :] = end[1, here, :] * (value - out_ha[n, here, :])

        buffers = solve(coef, buffers, hold, first_rhs, final)
    for p in range(planes):
        value = buffers[0][p, PAD : PAD + ny, :]
        if out_native:
            out_field[flipped(p, planes, parity)] = value
        else:
            out_field[p] = value


def neumann_kernel(lo, first, more, fresh, *refs):
    refs = list(refs)
    take = lambda n: [refs.pop(0) for _ in range(n)]
    (coef,) = take(1)
    _, _, position = place()
    q_a, q_b, got_a, got_b = take(4)
    if not first:
        (state,) = take(1)
    if fresh:
        (ng,) = take(1)
    if more:
        (out_state,) = take(1)
    out_a, out_b, va, vb, hold = take(5)
    planes = va.shape[0]
    steps, ny, nz = out_a.shape
    clear_pads((va, vb))
    if not first:
        for p in range(planes):
            va[p, PAD : PAD + ny, :] = state[p]
    buffers = [va, vb]
    for n in range(steps):
        zero = first and n == 0

        def first_rhs(p, here, x):
            value = jnp.zeros((8, nz), F32) if zero else coef[row_cap(p), here, :] * x
            if p == 0:
                jump = q_b[n, here, :] + got_b[n, here, :]
                value = value + coef[row_end(planes, 0), here, :] * jump
            if p == planes - 1:
                jump = q_a[n, here, :] + got_a[n, here, :]
                value = value + coef[row_end(planes, 1), here, :] * jump
            return value

        def final(p, here, value):
            if p == 0:
                out_b[n, here, :] = value
            if p == planes - 1:
                out_a[n, here, :] = value

        buffers = solve(coef, buffers, hold, first_rhs, final, known_zero=zero)
    if more:
        for p in range(planes):
            out_state[p] = buffers[0][p, PAD : PAD + ny, :]
    if fresh:
        groups = lax.axis_size("iter")
        begins = (-fresh - 1) % groups

        @pl.when(position == begins)
        def _():
            for n in range(steps):
                out_b[n] = ng[fresh - 1, 0, lo + n]


def correct_kernel(h_a, h_b, psi_a, psi_b, got_a, got_b, out):
    parity, _, _ = place()
    far = has_far()

    @pl.when(parity == 0)
    def _():
        out[...] = h_a[...] + 0.25 * (psi_a[...] + got_a[...])

    @pl.when(parity == 1)
    def _():
        out[...] = jnp.where(far, h_b[...] + 0.25 * (psi_b[...] + got_b[...]), 0.0)


def cut_kernel(whole, *outs):
    lo = 0
    for out in outs:
        for n in range(out.shape[0]):
            out[n] = whole[0, 0, lo + n]
        lo += out.shape[0]


def run(kernel, outs, args, scratch=(), smem=0):
    specs = [pl.BlockSpec(memory_space=pltpu.SMEM)] * smem
    specs += [pl.BlockSpec(memory_space=pltpu.VMEM)] * (len(args) - smem)
    many = isinstance(outs, tuple)
    return pl.pallas_call(
        kernel,
        out_shape=outs,
        in_specs=specs,
        out_specs=tuple([pl.BlockSpec(memory_space=pltpu.VMEM)] * len(outs)) if many else specs[-1],
        scratch_shapes=list(scratch),
        compiler_params=pltpu.CompilerParams(vmem_limit_bytes=LIMIT),
    )(*args[:smem], *[near(a) for a in args[smem:]])


def local(layout, fields, labels, traces, new_guess, cond_table, cap_table):
    return steps_of(layout, fields, labels, traces, new_guess, cond_table, cap_table)


def steps_of(layout, fields, labels, traces, new_guess, cond_table, cap_table):
    def move(value, pairs):
        return lax.ppermute(value, AXES, pairs)

    planes, ny, nz = labels.shape
    steps = traces.shape[2]
    ticks = new_guess.shape[0] + 1
    groups = layout.groups
    odd = lax.rem(lax.axis_index("sub"), 2)
    chunks = cuts(steps)
    scratch = [vmem((planes, ny + 2 * PAD, nz))] * 2 + [vmem((planes, ny, nz))]

    held = move(traces, layout.enter)
    labels = move(labels, layout.enter)
    field = move(fields, layout.enter)
    pieces = run(cut_kernel, tuple(vmem((hi - lo, ny, nz)) for lo, hi in chunks), [held])
    waves = {}
    for (lo, hi), piece in zip(chunks, pieces):
        waves[lo] = (piece, move(piece, layout.core), move(piece, layout.chip))
    count = rows(planes)
    dir_coef, neu_coef, end = run(
        setup_kernel,
        (vmem((count, ny, nz)), vmem((count, ny, nz)), vmem((2, ny, nz))),
        [cond_table, cap_table, labels],
        smem=2,
    )

    starts = {t: (-t - 1) % groups for t in range(1, ticks)}
    odds = [t for t in starts if starts[t] % 2]
    evens = [t for t in starts if starts[t] % 2 == 0]
    crossed = {}
    for n in range(max(len(odds), len(evens))):
        ours = odds[n] if n < len(odds) else evens[n]
        theirs = evens[n] if n < len(evens) else odds[n]
        message = jnp.where(odd == 0, new_guess[ours - 1, 0], new_guess[theirs - 1, 0])
        arrived = move(message, layout.guess)
        crossed[ours] = crossed[theirs] = arrived

    for tick in range(ticks):
        last = tick == ticks - 1
        sent = []
        for lo, hi in chunks:
            plane = vmem((hi - lo, ny, nz))
            field, q_a, q_b, h_a, h_b = run(
                functools.partial(dirichlet_kernel, lo, tick == 0, tick == 0 and lo == 0, tick, last and hi == steps),
                (vmem((planes, ny, nz)), plane, plane, plane, plane),
                [dir_coef, end, field, *waves[lo]] + ([new_guess, crossed[tick]] if tick else []),
                scratch,
            )
            in_a, in_b = move(q_a, layout.core), move(q_b, layout.chip)
            sent.append((q_a, q_b, in_a, in_b, h_a, h_b))
        if last:
            field = move(field[None], layout.home(ticks))
        else:
            field = move(field, layout.field)
        fresh = 0 if last else tick + 1
        state = []
        ends = []
        for n, ((lo, hi), (q_a, q_b, in_a, in_b, h_a, h_b)) in enumerate(zip(chunks, sent)):
            plane = vmem((hi - lo, ny, nz))
            more = n + 1 < len(chunks)
            swap = fresh if fresh and starts[fresh] % 2 else 0
            *state, psi_a, psi_b = run(
                functools.partial(neumann_kernel, lo, lo == 0, more, swap),
                ((vmem((planes, ny, nz)),) if more else ()) + (plane, plane),
                [neu_coef, q_a, q_b, in_a, in_b, *state] + ([new_guess] if swap else []),
                scratch,
            )
            in_a, in_b = move(psi_a, layout.core), move(psi_b, layout.chip)
            waves[lo] = (h_a, h_b, psi_a, psi_b, in_a, in_b)
            if last:
                done = run(correct_kernel, plane, list(waves[lo]))
                ends.append(move(done, layout.home(ticks)))
    corrected = ends[0] if len(ends) == 1 else jnp.concatenate(ends, axis=0)
    return field, corrected[None, None]


def cuts(steps):
    size = max(1, steps // SPLIT)
    return [(lo, min(lo + size, steps)) for lo in range(0, steps, size)]


def solution(mesh):
    layout = Layout(mesh.shape["sub"], mesh.shape["iter"])
    return jax.shard_map(
        functools.partial(local, layout),
        mesh=mesh,
        in_specs=(
            P("iter", "sub", None, None),
            P("sub", None, None),
            P("iter", "sub", None, None, None),
            P(None, "sub", None, None, None),
            P(),
            P(),
        ),
        out_specs=(P("iter", "sub", None, None), P("iter", "sub", None, None, None)),
        check_vma=False,
    )
```

```python
import functools

import jax
import jax.numpy as jnp
from jax import lax
from jax.experimental import pallas as pl
from jax.experimental.pallas import tpu as pltpu
from jax.sharding import PartitionSpec as P


SWEEPS = 3
AXES = ("sub", "iter")
F32 = jnp.float32
PAD = 8
SPLIT = 2
LIMIT = 8 << 20


def vmem(shape, dtype=F32):
    return pltpu.VMEM(shape, dtype)


def near(value):
    return pltpu.with_memory_space_constraint(value, pltpu.VMEM)


def harmonic(first, second):
    return 2.0 * first * second / (first + second)


class Layout:
    def __init__(self, slabs, groups):
        assert slabs % 2 == 0 and groups % 2 == 0
        self.slabs, self.groups = slabs, groups
        every = [(s, p) for s in range(slabs) for p in range(groups)]
        at = self.at
        self.core = [(at(s, p), at(s ^ 1, p)) for s, p in every]
        self.chip = []
        for s, p in every:
            t = s + 1 if s % 2 else s - 1
            self.chip.append((at(s, p), at(t, p) if 0 <= t < slabs else at(s, (p + 2) % groups)))
        self.field = [(at(s, p), at(s, (p - 1) % groups)) for s, p in every]
        self.enter = [(s * groups + g, at(s, (g - 1) % groups)) for s, g in every]

    def at(self, s, p):
        return (2 * (s // 2) + p % 2) * self.groups + 2 * (p // 2) + s % 2

    def home(self, ticks):
        every = [(s, p) for s in range(self.slabs) for p in range(self.groups)]
        return [(self.at(s, p), s * self.groups + (p + ticks) % self.groups) for s, p in every]


def place():
    sub, it = lax.axis_index("sub"), lax.axis_index("iter")
    parity = lax.rem(it, 2)
    slab = 2 * (sub // 2) + parity
    position = 2 * (it // 2) + lax.rem(sub, 2)
    return parity, slab, position


def has_far():
    parity, slab, _ = place()
    last = lax.axis_size("sub") - 1
    return jnp.logical_not(jnp.where(parity == 0, slab == 0, slab == last))


def flipped(plane, planes, parity):
    return plane + parity * (planes - 1 - 2 * plane)


def row_cap(p):
    return 5 * p


def row_face(planes, f):
    return 5 * planes + 2 * f


def row_end(planes, role_a):
    return 5 * planes + 2 * (planes - 1) + role_a


def rows(planes):
    return 5 * planes + 2 * (planes - 1) + 2


def setup_kernel(cond_ref, cap_ref, label_ref, dir_ref, neu_ref, end_ref):
    planes, ny, nz = label_ref.shape
    parity, _, _ = place()
    far = has_far()
    row = lax.broadcasted_iota(jnp.int32, (ny, nz), 0)
    col = lax.broadcasted_iota(jnp.int32, (ny, nz), 1)
    ks, cs = [], []
    for p in range(planes):
        at = flipped(p, planes, parity)
        label = label_ref[at]
        k = jnp.zeros((ny, nz), F32)
        c = jnp.zeros((ny, nz), F32)
        for cls in range(cond_ref.shape[0]):
            hit = label == cls
            k = jnp.where(hit, cond_ref[cls], k)
            c = jnp.where(hit, cap_ref[cls], c)
        ks.append(k)
        cs.append(c)
    faces = [harmonic(ks[f], ks[f + 1]) for f in range(planes - 1)]
    end_ref[0] = 2.0 * ks[0]
    end_ref[1] = 2.0 * ks[-1]
    for p in range(planes):
        k = ks[p]
        down = harmonic(k, pltpu.roll(k, ny - 1, 0))
        up = pltpu.roll(down, 1, 0)
        right = harmonic(k, pltpu.roll(k, nz - 1, 1))
        left = pltpu.roll(right, 1, 1)
        edge = 2.0 * k
        total = cs[p]
        total = total + ((faces[p - 1] if p else edge) + (faces[p] if p < planes - 1 else edge))
        total = total + (jnp.where(row == 0, edge, up) + jnp.where(row == ny - 1, edge, down))
        total = total + (jnp.where(col == 0, edge, left) + jnp.where(col == nz - 1, edge, right))
        up = jnp.where(row == 0, 0.0, up)
        down = jnp.where(row == ny - 1, 0.0, down)
        left = jnp.where(col == 0, 0.0, left)
        right = jnp.where(col == nz - 1, 0.0, right)
        free = total
        if p == 0:
            free = free - jnp.where(far, edge, 0.0)
        if p == planes - 1:
            free = free - edge
        for out, diag in ((dir_ref, total), (neu_ref, free)):
            inverse = 1.0 / diag
            for n, value in enumerate((cs[p], up, down, left, right)):
                out[row_cap(p) + n] = value * inverse
            if p < planes - 1:
                out[row_face(planes, p)] = faces[p] * inverse
            if p:
                out[row_face(planes, p - 1) + 1] = faces[p - 1] * inverse
            weight = edge * inverse if out is dir_ref else inverse
            if p == 0:
                out[row_end(planes, 0)] = jnp.where(far, weight, 0.0)
            if p == planes - 1:
                out[row_end(planes, 1)] = weight


def clear_pads(refs):
    for ref in refs:
        planes, tall, nz = ref.shape
        for p in range(planes):
            ref[p, 0:PAD, :] = jnp.zeros((PAD, nz), F32)
            ref[p, tall - PAD : tall, :] = jnp.zeros((PAD, nz), F32)


def sweep(coef, source, target, rhs):
    planes, tall, nz = source.shape
    for r in range(0, tall - 2 * PAD, 8):
        here = slice(r, r + 8)
        xs = [source[p, PAD + r : PAD + r + 8, :] for p in range(planes)]
        for p in range(planes):
            x = xs[p]
            base = row_cap(p)
            value = rhs(p, here, x)
            if p < planes - 1:
                value = value + coef[row_face(planes, p), here, :] * xs[p + 1]
            if p:
                value = value + coef[row_face(planes, p - 1) + 1, here, :] * xs[p - 1]
            side = coef[base + 1, here, :] * source[p, PAD + r - 1 : PAD + r + 7, :]
            side = side + coef[base + 2, here, :] * source[p, PAD + r + 1 : PAD + r + 9, :]
            value = value + side
            side = coef[base + 3, here, :] * pltpu.roll(x, 1, 1)
            side = side + coef[base + 4, here, :] * pltpu.roll(x, nz - 1, 1)
            target(p, here, value + side)


def padded(here):
    return slice(here.start + PAD, here.stop + PAD)


def solve(coef, buffers, hold, first_rhs, final, known_zero=False):
    planes, tall, _ = buffers[0].shape

    for n in range(SWEEPS):
        source, target = buffers

        def rhs(p, here, x):
            if n:
                return hold[p, here, :]
            value = first_rhs(p, here, x)
            hold[p, here, :] = value
            return value

        def put(p, here, value):
            target[p, padded(here), :] = value
            if n == SWEEPS - 1:
                final(p, here, value)

        if n == 0 and known_zero:
            for r in range(0, tall - 2 * PAD, 8):
                for p in range(planes):
                    here = slice(r, r + 8)
                    put(p, here, rhs(p, here, None))
        else:
            sweep(coef, source, put, rhs)
        buffers = buffers[::-1]
    return buffers


def dirichlet_kernel(lo, start, enter, fresh, out_native, *refs):
    refs = list(refs)
    take = lambda n: [refs.pop(0) for _ in range(n)]
    coef, end, field = take(3)
    parity, _, position = place()
    far = has_far()
    if lo:
        (before,) = take(1)
    if start:
        held, from_core, from_chip = take(3)
    else:
        old_a, old_b, psi_a, psi_b, got_a, got_b, ng, gy = take(8)
    out_field, out_qa, out_qb, out_ha, out_hb, va, vb, hold = take(8)
    planes = va.shape[0]
    steps, ny, _ = out_qb.shape
    clear_pads((va, vb))
    for p in range(planes):
        value = field[0, flipped(p, planes, parity)] if enter else field[p]
        va[p, PAD : PAD + ny, :] = value
    for n in range(lo):
        out_qa[n] = before[n]
    for n in range(steps):
        if start:
            h_a = jnp.where(parity == 0, held[0, 0, lo + n], from_core[0, 0, lo + n])
            h_b = jnp.where(parity == 0, from_chip[n], held[0, 0, lo + n])
        else:
            h_a = old_a[n] + 0.25 * (psi_a[lo + n] + got_a[lo + n])
            h_b = old_b[n] + 0.25 * (psi_b[n] + got_b[n])
            groups = lax.axis_size("iter")
            begins = (-1 - fresh) % groups
            new = position == begins
            local, crossed = ng[fresh - 1, 0, lo + n], gy[lo + n]
            if begins % 2:
                new_a = jnp.where(parity == 0, crossed, got_a[lo + n])
                new_b = jnp.where(parity == 1, local, got_b[n])
            else:
                new_a = local
                new_b = jnp.where(parity == 1, crossed, got_b[n])
            h_a = jnp.where(new, new_a, h_a)
            h_b = jnp.where(new, new_b, h_b)
        out_ha[n] = h_a
        out_hb[n] = jnp.where(far, h_b, 0.0)
    buffers = [va, vb]
    for n in range(steps):

        def first_rhs(p, here, x):
            value = coef[row_cap(p), here, :] * x
            if p == 0:
                value = value + coef[row_end(planes, 0), here, :] * out_hb[n, here, :]
            if p == planes - 1:
                value = value + coef[row_end(planes, 1), here, :] * out_ha[n, here, :]
            return value

        def final(p, here, value):
            if p == 0:
                out_qb[n, here, :] = end[0, here, :] * (value - out_hb[n, here, :])
            if p == planes - 1:
                out_qa[lo + n, here, :] = end[1, here, :] * (value - out_ha[n, here, :])

        buffers = solve(coef, buffers, hold, first_rhs, final)
    for p in range(planes):
        value = buffers[0][p, PAD : PAD + ny, :]
        if out_native:
            out_field[flipped(p, planes, parity)] = value
        else:
            out_field[p] = value


def neumann_kernel(lo, more, fresh, *refs):
    refs = list(refs)
    take = lambda n: [refs.pop(0) for _ in range(n)]
    coef, q_a, q_b, got_a, got_b = take(5)
    _, _, position = place()
    if lo:
        state, before = take(2)
    if fresh:
        ng, gy = take(2)
    if more:
        (out_state,) = take(1)
    out_a, out_b, va, vb, hold = take(5)
    planes = va.shape[0]
    steps, ny, nz = out_b.shape
    clear_pads((va, vb))
    if lo:
        for p in range(planes):
            va[p, PAD : PAD + ny, :] = state[p]
        for n in range(lo):
            out_a[n] = before[n]
    buffers = [va, vb]
    for n in range(steps):
        zero = lo == 0 and n == 0

        def first_rhs(p, here, x):
            value = jnp.zeros((8, nz), F32) if zero else coef[row_cap(p), here, :] * x
            if p == 0:
                jump = q_b[n, here, :] + got_b[n, here, :]
                value = value + coef[row_end(planes, 0), here, :] * jump
            if p == planes - 1:
                jump = q_a[lo + n, here, :] + got_a[lo + n, here, :]
                value = value + coef[row_end(planes, 1), here, :] * jump
            return value

        def final(p, here, value):
            if p == 0:
                out_b[n, here, :] = value
            if p == planes - 1:
                out_a[lo + n, here, :] = value

        buffers = solve(coef, buffers, hold, first_rhs, final, known_zero=zero)
    if more:
        for p in range(planes):
            out_state[p] = buffers[0][p, PAD : PAD + ny, :]
    if fresh:
        groups = lax.axis_size("iter")
        begins = (-1 - fresh) % groups

        @pl.when(position == begins)
        def _():
            for n in range(steps):
                if begins % 2:
                    out_a[lo + n] = gy[lo + n]
                    out_b[n] = ng[fresh - 1, 0, lo + n]
                else:
                    out_b[n] = gy[lo + n]


def correct_kernel(lo, h_a, h_b, psi_a, psi_b, got_a, got_b, out):
    parity, _, _ = place()
    far = has_far()

    @pl.when(parity == 0)
    def _():
        for n in range(out.shape[0]):
            out[n] = h_a[n] + 0.25 * (psi_a[lo + n] + got_a[lo + n])

    @pl.when(parity == 1)
    def _():
        for n in range(out.shape[0]):
            out[n] = jnp.where(far, h_b[n] + 0.25 * (psi_b[n] + got_b[n]), 0.0)


def cut_kernel(whole, *outs):
    lo = 0
    for out in outs:
        for n in range(out.shape[0]):
            out[n] = whole[0, 0, lo + n]
        lo += out.shape[0]


def pick_kernel(picks, guess, *messages):
    even = lax.rem(lax.axis_index("iter"), 2)
    for (for_odd, for_even), message in zip(picks, messages):
        for parity, tick in ((0, for_odd), (1, for_even)):

            @pl.when(even == parity)
            def _():
                message[...] = guess[tick - 1, 0]


def land_kernel(*refs):
    *pieces, out, sem = refs
    copies = []
    lo = 0
    for n, piece in enumerate(pieces):
        copies.append(pltpu.make_async_copy(piece, out.at[lo : lo + piece.shape[0]], sem.at[n]))
        copies[-1].start()
        lo += piece.shape[0]
    for copy in copies:
        copy.wait()


def land(pieces):
    shape = (sum(piece.shape[0] for piece in pieces),) + pieces[0].shape[1:]
    return pl.pallas_call(
        land_kernel,
        out_shape=jax.ShapeDtypeStruct(shape, F32),
        in_specs=[pl.BlockSpec(memory_space=pltpu.VMEM)] * len(pieces),
        out_specs=pl.BlockSpec(memory_space=pl.ANY),
        scratch_shapes=[pltpu.SemaphoreType.DMA((len(pieces),))],
        compiler_params=pltpu.CompilerParams(vmem_limit_bytes=LIMIT),
    )(*[near(piece) for piece in pieces])


def run(kernel, outs, args, scratch=(), smem=0, bring=True):
    specs = [pl.BlockSpec(memory_space=pltpu.SMEM)] * smem
    specs += [pl.BlockSpec(memory_space=pltpu.VMEM)] * (len(args) - smem)
    many = isinstance(outs, tuple)
    return pl.pallas_call(
        kernel,
        out_shape=outs,
        in_specs=specs,
        out_specs=tuple([pl.BlockSpec(memory_space=pltpu.VMEM)] * len(outs)) if many else specs[-1],
        scratch_shapes=list(scratch),
        compiler_params=pltpu.CompilerParams(vmem_limit_bytes=LIMIT),
    )(*args[:smem], *[near(a) if bring else a for a in args[smem:]])


def local(layout, fields, labels, traces, new_guess, cond_table, cap_table):
    return steps_of(layout, fields, labels, traces, new_guess, cond_table, cap_table)


def steps_of(layout, fields, labels, traces, new_guess, cond_table, cap_table):
    def move(value, pairs):
        return lax.ppermute(value, AXES, pairs)

    planes, ny, nz = labels.shape
    steps = traces.shape[2]
    ticks = new_guess.shape[0] + 1
    groups = layout.groups
    chunks = cuts(steps)
    scratch = [vmem((planes, ny + 2 * PAD, nz))] * 2 + [vmem((planes, ny, nz))]

    held = move(traces, layout.enter)
    labels = move(labels, layout.enter)
    field = move(fields, layout.enter)
    if len(chunks) > 1:
        pieces = run(cut_kernel, tuple(vmem((hi - lo, ny, nz)) for lo, hi in chunks), [held])
    else:
        pieces = [held[0, 0]]
    from_chip = {lo: move(piece, layout.chip) for (lo, _), piece in zip(chunks, pieces)}
    from_core = move(held, layout.core)
    count = rows(planes)
    dir_coef, neu_coef, end = run(
        setup_kernel,
        (vmem((count, ny, nz)), vmem((count, ny, nz)), vmem((2, ny, nz))),
        [cond_table, cap_table, labels],
        smem=2,
    )

    starts = {t: (-1 - t) % groups for t in range(1, ticks)}
    odds = [t for t in starts if starts[t] % 2]
    evens = [t for t in starts if starts[t] % 2 == 0]
    picks = []
    for n in range(max(len(odds), len(evens))):
        picks.append((odds[n] if n < len(odds) else evens[n], evens[n] if n < len(evens) else odds[n]))
    crossed = {}
    messages = run(functools.partial(pick_kernel, picks), tuple(vmem((steps, ny, nz)) for _ in picks), [new_guess])
    for served, message in zip(picks, messages):
        arrived = move(message, layout.enter)
        for t in served:
            crossed[t] = arrived

    waves = {}
    for tick in range(ticks):
        last = tick == ticks - 1
        sent = []
        q_a = None
        for lo, hi in chunks:
            plane = vmem((hi - lo, ny, nz))
            traces_in = [held, from_core, from_chip[lo]] if tick == 0 else [*waves[lo], new_guess, crossed[tick]]
            field, q_a, q_b, h_a, h_b = run(
                functools.partial(dirichlet_kernel, lo, tick == 0, tick == 0 and lo == 0, tick, last and hi == steps),
                (vmem((planes, ny, nz)), vmem((hi, ny, nz)), plane, plane, plane),
                [dir_coef, end, field] + ([q_a] if lo else []) + traces_in,
                scratch,
            )
            sent.append((q_b, move(q_b, layout.chip), h_a, h_b))
        in_a = move(q_a, layout.core)
        if last:
            field = move(field, layout.home(ticks))
        else:
            field = move(field, layout.field)
        fresh = 0 if last else tick + 1
        state = []
        psi = []
        for (lo, hi), (q_b, in_b, h_a, h_b) in zip(chunks, sent):
            plane = vmem((hi - lo, ny, nz))
            more = hi < steps
            *state, psi_a, psi_b = run(
                functools.partial(neumann_kernel, lo, more, fresh),
                ((vmem((planes, ny, nz)),) if more else ()) + (vmem((hi, ny, nz)), plane),
                [neu_coef, q_a, q_b, in_a, in_b] + (state + [psi_a] if lo else []) + ([new_guess, crossed[fresh]] if fresh else []),
                scratch,
            )
            psi.append((psi_b, move(psi_b, layout.chip), h_a, h_b))
        got_a = move(psi_a, layout.core)
        ends = []
        for (lo, hi), (psi_b, got_b, h_a, h_b) in zip(chunks, psi):
            waves[lo] = (h_a, h_b, psi_a, psi_b, got_a, got_b)
            if last:
                plane = vmem((hi - lo, ny, nz))
                done = run(functools.partial(correct_kernel, lo), plane, list(waves[lo]))
                ends.append(move(done, layout.home(ticks)))
    return land([field])[None], land(ends)[None, None]


def cuts(steps):
    size = max(1, steps // SPLIT)
    return [(lo, min(lo + size, steps)) for lo in range(0, steps, size)]


def solution(mesh):
    layout = Layout(mesh.shape["sub"], mesh.shape["iter"])
    return jax.shard_map(
        functools.partial(local, layout),
        mesh=mesh,
        in_specs=(
            P("iter", "sub", None, None),
            P("sub", None, None),
            P("iter", "sub", None, None, None),
            P(None, "sub", None, None, None),
            P(),
            P(),
        ),
        out_specs=(P("iter", "sub", None, None), P("iter", "sub", None, None, None)),
        check_vma=False,
    )
```
